32 devices in a mesh: seq: 4 (over z), batch: 8 (over y, x, core).
Axes of the slice: x: 2, y: 2, z: 4, core: 2. Of those that a mesh axis runs over, the one named last changes fastest.
Arguments:
- queries: bfloat16 [8, 1024, 1024], P('batch', 'seq'), may hold values from -80 to 80
- keys: bfloat16 [8, 1024, 1024], P('batch', 'seq'), may hold values from -8 to 8
- values: bfloat16 [8, 1024, 1024], P('batch', 'seq'), may hold values from -6 to 6
- residual: bfloat16 [8, 1024, 1024], P('batch', 'seq'), may hold values from -2 to 2
- out_weight: bfloat16 [1024, 1024], replicated, may hold values from -0.1875 to 0.1875
- norm_gain: float32 [1024], replicated, may hold values from 0.1 to 1.9
- source_queue: bfloat16 [4096, 1024], P('batch'), may hold values from -32 to 32
- span_lengths: int32 [8, 64], P('batch'), may hold values from 1 to 32, 1024 in all within a row
- positives: int32 [8, 64], P(None, 'seq'), may hold values from 0 to 4095
Outputs:
- anchors: bfloat16 [8, 64, 1024], P('batch', 'seq')
- losses: float32 [8, 64], P('batch', 'seq')
The draws below stay inside these ranges and needn't reach their ends.
All inputs are finite; a program needn't handle non-finite values.
Results may differ from the reference program's by a relative error of at most 0.0047.
Values may be sent and summed in bfloat16 or wider, within the bound.
A program may use at most 64 MiB of HBM per device.

```python
import math
import jax
import jax.numpy as jnp
import numpy as np
from jax import lax

D = 1024
HEADS = 16
HEAD_DIM = 64
WINDOW = 512
FUNC_DEV = 16
BINARIES = 8
LENGTH = 1024
FUNCS = 64
FN_MOST = 32
QUEUE = 4096
N_SEQ = 4


def draw_pair(key):
    pair_key = jax.random.fold_in(key, 11)
    key_query, key_key = jax.random.split(pair_key, 2)
    full_shape = (BINARIES, LENGTH, D)
    query_part = jnp.clip(jax.random.normal(key_query, full_shape, jnp.float32), -6.0, 6.0)
    key_part = jnp.clip(jax.random.normal(key_key, full_shape, jnp.float32), -6.0, 6.0)
    return (query_part, key_part)


def draw_queries(key, part):
    return draw_pair(key)[0].astype(jnp.bfloat16)


def draw_keys(key, part):
    return draw_pair(key)[1].astype(jnp.bfloat16)


def draw_source_queue(key, part):
    key_rows = jax.random.fold_in(jax.random.fold_in(key, 23), 0)
    key_entries = jax.random.fold_in(jax.random.fold_in(key, 23), 2)
    row_scale = jnp.exp(jax.random.uniform(key_rows, (QUEUE, 1), jnp.float32, math.log(0.05), math.log(0.5)))
    entries = jnp.clip(jax.random.normal(key_entries, (QUEUE, D), jnp.float32), -6.0, 6.0)
    return (entries * row_scale).astype(jnp.bfloat16)


def set_ends(values, key, smallest, largest):
    longest = values.shape.index(max(values.shape))
    spots = []
    for shift in (0, 1):
        where = [jax.random.randint(jax.random.fold_in(key, axis), (), 0, length) for axis, length in enumerate(values.shape)]
        where[longest] = (where[longest] + shift) % values.shape[longest]
        spots.append(tuple(where))
    return values.at[spots[0]].set(smallest).at[spots[1]].set(largest)


def steps_of(stream_key, extent, shards, least, high):
    factor_of, own = 1.0, jax.random.fold_in(stream_key, 6)
    for axis_at, blocks in shards:
        draws = jnp.exp(jax.random.uniform(jax.random.fold_in(own, axis_at), (blocks,), jnp.float32, least / len(shards), high / len(shards)))
        factor_of = factor_of * jnp.repeat(draws, extent[axis_at] // blocks).reshape([-1 if axis == axis_at else 1 for axis in range(len(extent))])
    return factor_of


def profile(number_of, total, limit, slope):
    portions = [(1 << 20) // math.isqrt(rank ** slope) + 1 for rank in range(2, number_of + 1)]
    surplus, holding = total - limit - (number_of - 1), [1] * (number_of - 1)
    while surplus > 0:
        free = [i for i in range(number_of - 1) if holding[i] < limit]
        whole, budget = sum([portions[i] for i in free]), surplus
        for i in free:
            more = min(limit - holding[i], max(1, budget * portions[i] // whole), surplus)
            holding[i] = holding[i] + more
            surplus = surplus - more
    return np.array([limit] + holding)


def uneven_parts(rng, amount, total, most, skew):
    if amount == 2:
        one = jax.random.randint(rng, (), max(1, total - most), min(most, total - 1) + 1)
        return jnp.stack([one, total - one])
    sizes = jnp.asarray(profile(amount, total, most, skew), jnp.int32)
    twos = (amount - 1) // 2
    giver, receiver = sizes[1:1 + 2 * twos:2], sizes[2:2 + 2 * twos:2]
    slack = jnp.minimum(giver - 1, most - receiver)
    moved = jax.random.randint(jax.random.fold_in(rng, 1), (twos,), 0, 1 << 20) % (slack + 1)
    sizes = sizes.at[1:1 + 2 * twos:2].set(giver - moved).at[2:2 + 2 * twos:2].set(receiver + moved)
    return sizes[jax.random.permutation(jax.random.fold_in(rng, 2), amount)]


def normal_values(stream_key, shape, width, most, cuts=(), kind=jnp.bfloat16):
    drawn = jax.random.normal(stream_key, shape, jnp.float32) * width
    if len(cuts) > 0:
        drawn = steps_of(stream_key, shape, cuts, -0.22, 0.18) * drawn
    return jnp.clip(drawn, min=-most, max=most).astype(kind)


def setup_inputs(seed: int = 0) -> dict:
    streams_of = jax.random.split(jax.random.key(seed), 10)
    queries = draw_queries(jax.random.fold_in(streams_of[9], 71), 0)
    keys = draw_keys(jax.random.fold_in(streams_of[9], 71), 0)
    values = normal_values(streams_of[2], (BINARIES, LENGTH, D), 1.0, 6.0, ((0, 8), (1, 4)))
    residual = normal_values(streams_of[3], (BINARIES, LENGTH, D), 0.25, 2.0, ((0, 8), (1, 4)))
    out_weight = normal_values(streams_of[4], (D, D), D ** -0.5, 0.1875)
    norm_gain = jnp.clip(1.0 + 0.18 * jax.random.normal(streams_of[5], (D,), jnp.float32), 0.1, 1.9)
    source_queue = draw_source_queue(jax.random.fold_in(streams_of[9], 71), 0)
    span_lengths = jax.vmap(lambda own: uneven_parts(own, FUNCS, LENGTH, FN_MOST, 2))(jax.random.split(streams_of[7], BINARIES)).reshape((BINARIES, FUNCS)).astype(jnp.int32)
    positives = set_ends(jax.random.randint(streams_of[8], (BINARIES, FUNCS), 0, QUEUE), jax.random.fold_in(streams_of[8], 1), 0, QUEUE - 1).astype(jnp.int32)
    return {"queries": queries, "keys": keys, "values": values, "residual": residual, "out_weight": out_weight, "norm_gain": norm_gain, "source_queue": source_queue, "span_lengths": span_lengths, "positives": positives}


def attend(queries, keys, values):
    block_rows = math.gcd(LENGTH, 512)
    padded_keys = jnp.pad(keys, ((WINDOW, 0), (0, 0)))
    padded_values = jnp.pad(values, ((WINDOW, 0), (0, 0)))

    def one_block(block_index):
        first_row = block_index * block_rows
        query_block = lax.dynamic_slice(queries, (first_row, jnp.int32(0)), (block_rows, D))
        key_block = lax.dynamic_slice(padded_keys, (first_row, jnp.int32(0)), (block_rows + WINDOW, D))
        value_block = lax.dynamic_slice(padded_values, (first_row, jnp.int32(0)), (block_rows + WINDOW, D))
        query_pos = first_row + jnp.arange(block_rows, dtype=jnp.int32)
        key_pos = first_row - WINDOW + jnp.arange(block_rows + WINDOW, dtype=jnp.int32)
        distance = query_pos[:, None] - key_pos[None, :]
        allowed = (distance >= 0) & (distance < WINDOW) & (key_pos[None, :] >= 0)
        query_heads = query_block.reshape(block_rows, HEADS, HEAD_DIM).astype(jnp.float32)
        key_heads = key_block.reshape(block_rows + WINDOW, HEADS, HEAD_DIM).astype(jnp.float32)
        value_heads = value_block.reshape(block_rows + WINDOW, HEADS, HEAD_DIM).astype(jnp.float32)
        scores = jnp.einsum('qhd,khd->hqk', query_heads, key_heads) / math.sqrt(HEAD_DIM)
        scores = jnp.where(allowed[None], scores, -jnp.inf)
        row_peak = lax.optimization_barrier(jnp.max(scores, axis=-1, keepdims=True))
        exp_scores = jnp.exp(scores - row_peak)
        weights = (exp_scores / lax.optimization_barrier(jnp.sum(exp_scores, axis=-1, keepdims=True))).astype(jnp.bfloat16)
        mixed = jnp.einsum('hqk,khd->qhd', weights.astype(jnp.float32), value_heads)
        return mixed.astype(jnp.bfloat16).reshape(block_rows, D)
    blocks = lax.map(one_block, jnp.arange(LENGTH // block_rows, dtype=jnp.int32))
    return blocks.reshape(LENGTH, D)

def reference(queries, keys, values, residual, out_weight, norm_gain, source_queue, span_lengths, positives):

    def per_binary(binary_items):
        query_rows, key_rows, value_rows, stream, lengths, wanted = binary_items
        attended = attend(query_rows, key_rows, value_rows)
        hidden = stream.astype(jnp.float32) + jnp.dot(attended, out_weight, preferred_element_type=jnp.float32)
        scale = lax.rsqrt(lax.optimization_barrier(jnp.mean(hidden * hidden, axis=-1, keepdims=True)) + 1e-05)
        normed = (hidden * scale * norm_gain.astype(jnp.float32)).astype(jnp.bfloat16)
        span_ends = jnp.cumsum(lengths).astype(jnp.int32)
        starts = span_ends - lengths
        row_ids = jnp.arange(FUNCS, dtype=jnp.int32)
        listed = (row_ids % FUNC_DEV * N_SEQ + row_ids // FUNC_DEV).astype(jnp.int32)
        row_starts = jnp.take(starts, listed)
        row_ends = jnp.take(span_ends, listed)
        token_pos = jnp.arange(LENGTH, dtype=jnp.int32)
        member = ((token_pos[None, :] >= row_starts[:, None]) & (token_pos[None, :] < row_ends[:, None])).astype(jnp.bfloat16)
        pooled = jnp.dot(member, normed, preferred_element_type=jnp.float32)
        anchor_rows = (pooled * lax.rsqrt(lax.optimization_barrier(jnp.sum(pooled * pooled, axis=-1, keepdims=True)) + 1e-06)).astype(jnp.bfloat16)
        logits = 20.0 * jnp.dot(anchor_rows, source_queue.T, preferred_element_type=jnp.float32)
        row_peak = lax.optimization_barrier(jnp.max(logits, axis=-1))
        log_total = row_peak + jnp.log(lax.optimization_barrier(jnp.sum(jnp.exp(logits - row_peak[:, None]), axis=-1)))
        positive = jnp.take_along_axis(logits, wanted[:, None].astype(jnp.int32), axis=1)[:, 0]
        return (anchor_rows, log_total - positive)
    anchors, losses = lax.map(per_binary, (queries, keys, values, residual, span_lengths, positives))
    return (anchors, losses)
```

```python
import functools
import math

import jax
import jax.numpy as jnp
from jax import lax
from jax.experimental import pallas as pl
from jax.experimental.pallas import tpu as pltpu
from jax.sharding import PartitionSpec as P

HEADS = 16
WINDOW = 512
MESH = pl.DeviceIdType.MESH
F32 = jnp.float32
BF16 = jnp.bfloat16


logit_scale = 20.0


def shifted(array, axis, by):
    devices = lax.axis_size(axis)
    pairs = [(i, i + by) for i in range(devices) if 0 <= i + by < devices]
    return lax.ppermute(array, axis, pairs)


def tail_kernel(
    n_seq,
    n_batch,
    attended_ref,
    residual_ref,
    gain_ref,
    lengths_ref,
    wanted_ref,
    weight_hbm,
    queue_hbm,
    anchors_ref,
    losses_ref,
    weight,
    queue,
    parts,
    parts_in,
    anchors_all,
    stats,
    load_sem,
    part_send,
    part_recv,
    anchor_send,
    anchor_recv,
    stat_send,
    stat_recv,
):
    seq = lax.axis_index("seq")
    batch = lax.axis_index("batch")
    weight_load = pltpu.make_async_copy(weight_hbm, weight, load_sem.at[0])
    queue_load = pltpu.make_async_copy(queue_hbm, queue, load_sem.at[1])
    weight_load.start()
    queue_load.start()
    seq_peers = [lax.rem(seq + d, n_seq) for d in range(1, n_seq)]
    batch_peers = [lax.rem(batch + d, n_batch) for d in range(1, n_batch)]
    barrier = pltpu.get_barrier_semaphore()
    for peer in seq_peers:
        pl.semaphore_signal(barrier, inc=1, device_id={"seq": peer}, device_id_type=MESH)
    for peer in batch_peers:
        pl.semaphore_signal(barrier, inc=1, device_id={"batch": peer}, device_id_type=MESH)

    tok_rows = attended_ref.shape[0]
    own_rows, width = anchors_ref.shape
    funcs = own_rows * n_seq
    weight_load.wait()
    hidden = residual_ref[...].astype(F32) + jnp.dot(
        attended_ref[...], weight[...], preferred_element_type=F32
    )
    scale = lax.rsqrt(jnp.mean(hidden * hidden, axis=-1, keepdims=True) + 1e-05)
    normed = (hidden * scale * gain_ref[...]).astype(BF16)

    row_ids = lax.broadcasted_iota(jnp.int32, (funcs, funcs), 0)
    func_ids = lax.broadcasted_iota(jnp.int32, (funcs, funcs), 1)
    listed = lax.rem(row_ids, own_rows) * n_seq + row_ids // own_rows
    lengths = jnp.broadcast_to(lengths_ref[...].astype(F32), (funcs, funcs))
    begin_at = jnp.sum(jnp.where(func_ids < listed, lengths, 0.0), axis=1, keepdims=True)
    end_at = jnp.sum(jnp.where(func_ids <= listed, lengths, 0.0), axis=1, keepdims=True)
    pos = (
        seq * tok_rows + lax.broadcasted_iota(jnp.int32, (funcs, tok_rows), 1)
    ).astype(F32)
    member = jnp.where((pos >= begin_at) & (pos < end_at), 1.0, 0.0).astype(BF16)
    partial = jnp.dot(member, normed, preferred_element_type=F32)
    parts[...] = partial.reshape(n_seq, own_rows, width).astype(BF16)

    pl.semaphore_wait(barrier, n_seq - 1 + n_batch - 1)
    copies = []
    for d in range(1, n_seq):
        copy = pltpu.make_async_remote_copy(
            src_ref=parts.at[seq_peers[d - 1]],
            dst_ref=parts_in.at[d - 1],
            send_sem=part_send.at[d - 1],
            recv_sem=part_recv.at[d - 1],
            device_id={"seq": seq_peers[d - 1]},
            device_id_type=MESH,
        )
        copy.start()
        copies.append(copy)
    pooled = parts[seq].astype(F32)
    for d in range(1, n_seq):
        copies[d - 1].wait_recv()
        pooled = pooled + parts_in[d - 1].astype(F32)
    anchors = (
        pooled * lax.rsqrt(jnp.sum(pooled * pooled, axis=-1, keepdims=True) + 1e-06)
    ).astype(BF16)
    anchors_ref[...] = anchors
    anchors_all[batch] = anchors
    for copy in copies:
        copy.wait_send()

    copies = []
    for d in range(1, n_batch):
        copy = pltpu.make_async_remote_copy(
            src_ref=anchors_all.at[batch],
            dst_ref=anchors_all.at[batch],
            send_sem=anchor_send.at[d - 1],
            recv_sem=anchor_recv.at[d - 1],
            device_id={"batch": batch_peers[d - 1]},
            device_id_type=MESH,
        )
        copy.start()
        copies.append(copy)
    queue_load.wait()
    for copy in copies:
        copy.wait()
    rows = n_batch * own_rows
    logits = logit_scale * lax.dot_general(
        queue[...],
        anchors_all[...].reshape(rows, width),
        (((1,), (1,)), ((), ())),
        preferred_element_type=F32,
    )
    queue_rows = queue.shape[0]
    queue_ids = batch * queue_rows + lax.broadcasted_iota(jnp.int32, logits.shape, 0)
    row_peak = jnp.max(logits, axis=0, keepdims=True)
    row_total = jnp.sum(jnp.exp(logits - row_peak), axis=0, keepdims=True)
    positive = jnp.sum(
        jnp.where(wanted_ref[...] == queue_ids, logits, 0.0), axis=0, keepdims=True
    )
    stats[batch] = jnp.concatenate(
        [row_peak, row_total, positive, jnp.zeros((5, rows), F32)], axis=0
    )
    copies = []
    for d in range(1, n_batch):
        copy = pltpu.make_async_remote_copy(
            src_ref=stats.at[batch],
            dst_ref=stats.at[batch],
            send_sem=stat_send.at[d - 1],
            recv_sem=stat_recv.at[d - 1],
            device_id={"batch": batch_peers[d - 1]},
            device_id_type=MESH,
        )
        copy.start()
        copies.append(copy)
    for copy in copies:
        copy.wait()
    peaks = [stats[b, 0:1, :] for b in range(n_batch)]
    top = functools.reduce(jnp.maximum, peaks)
    total = sum(stats[b, 1:2, :] * jnp.exp(peaks[b] - top) for b in range(n_batch))
    chosen = sum(stats[b, 2:3, :] for b in range(n_batch))
    loss = top + jnp.log(total) - chosen
    loss_col = jnp.sum(
        jnp.where(
            lax.broadcasted_iota(jnp.int32, (own_rows, rows), 1)
            == batch * own_rows + lax.broadcasted_iota(jnp.int32, (own_rows, rows), 0),
            jnp.broadcast_to(loss, (own_rows, rows)),
            0.0,
        ),
        axis=1,
        keepdims=True,
    )
    losses_ref[...] = jnp.broadcast_to(loss_col, losses_ref.shape)


def tail(n_seq, n_batch, attended, residual, gain, lengths, wanted, weight, queue, own_rows):
    width = attended.shape[1]
    rows = n_batch * own_rows
    vmem = pl.BlockSpec(memory_space=pltpu.VMEM)
    hbm = pl.BlockSpec(memory_space=pl.ANY)
    return pl.pallas_call(
        functools.partial(tail_kernel, n_seq, n_batch),
        out_shape=(
            jax.ShapeDtypeStruct((own_rows, width), BF16),
            jax.ShapeDtypeStruct((own_rows, 128), F32),
        ),
        in_specs=[vmem] * 5 + [hbm] * 2,
        out_specs=(vmem, vmem),
        scratch_shapes=[
            pltpu.VMEM(weight.shape, BF16),
            pltpu.VMEM(queue.shape, BF16),
            pltpu.VMEM((n_seq, own_rows, width), BF16),
            pltpu.VMEM((n_seq - 1, own_rows, width), BF16),
            pltpu.VMEM((n_batch, own_rows, width), BF16),
            pltpu.VMEM((n_batch, 8, rows), F32),
            pltpu.SemaphoreType.DMA((2,)),
            pltpu.SemaphoreType.DMA((n_seq - 1,)),
            pltpu.SemaphoreType.DMA((n_seq - 1,)),
            pltpu.SemaphoreType.DMA((n_batch - 1,)),
            pltpu.SemaphoreType.DMA((n_batch - 1,)),
            pltpu.SemaphoreType.DMA((n_batch - 1,)),
            pltpu.SemaphoreType.DMA((n_batch - 1,)),
        ],
        compiler_params=pltpu.CompilerParams(
            collective_id=0, has_side_effects=True, vmem_limit_bytes=40 * 1024 * 1024
        ),
        name="tail",
    )(attended, residual, gain, lengths, wanted, weight, queue)


def body(
    queries, keys, values, residual, out_weight, norm_gain, source_queue, span_lengths, positives
):
    tok_rows = queries.shape[1]
    model_width = queries.shape[2]
    head_count = HEADS
    head_size = model_width // head_count
    reach_back = (WINDOW - 1) // tok_rows + 1
    seq_index = lax.axis_index("seq")
    first_pos = seq_index * tok_rows
    own_pair = jnp.stack([keys[0], values[0]])
    earlier = []
    for hop_count in range(1, reach_back + 1):
        earlier.append(shifted(own_pair, "seq", hop_count))
    ordered = earlier[::-1] + [own_pair]
    keys_all = jnp.concatenate([item[0] for item in ordered], axis=0)
    values_all = jnp.concatenate([item[1] for item in ordered], axis=0)
    query_pos = first_pos + jnp.arange(tok_rows, dtype=jnp.int32)
    key_pos = (
        first_pos - reach_back * tok_rows + jnp.arange((reach_back + 1) * tok_rows, dtype=jnp.int32)
    )
    distance = query_pos[:, None] - key_pos[None, :]
    allowed = (distance >= 0) & (distance < WINDOW) & (key_pos[None, :] >= 0)
    group_size = 4
    group_cols = group_size * head_size
    key_rows = keys_all.shape[0]

    def attend_group(group_index):
        first_col = group_index * group_cols
        query_group = lax.dynamic_slice_in_dim(queries[0], first_col, group_cols, 1).reshape(
            tok_rows, group_size, head_size
        )
        key_group = lax.dynamic_slice_in_dim(keys_all, first_col, group_cols, 1).reshape(
            key_rows, group_size, head_size
        )
        value_group = lax.dynamic_slice_in_dim(values_all, first_col, group_cols, 1).reshape(
            key_rows, group_size, head_size
        )
        scores = jnp.einsum(
            "qhd,khd->hqk", query_group, key_group, preferred_element_type=jnp.float32
        ) / math.sqrt(head_size)
        scores = jnp.where(allowed[None], scores, -jnp.inf)
        row_peak = jnp.max(scores, axis=-1, keepdims=True)
        exp_scores = jnp.exp(scores - row_peak)
        weights = (exp_scores / jnp.sum(exp_scores, axis=-1, keepdims=True)).astype(jnp.bfloat16)
        mixed = jnp.einsum("hqk,khd->qhd", weights, value_group, preferred_element_type=jnp.float32)
        return mixed.astype(jnp.bfloat16).reshape(tok_rows, group_cols)

    blocks = lax.map(attend_group, jnp.arange(head_count // group_size, dtype=jnp.int32))
    attended = jnp.transpose(blocks, (1, 0, 2)).reshape(tok_rows, model_width)
    own_rows = positives.shape[1]
    anchors, losses = tail(
        lax.axis_size("seq"),
        lax.axis_size("batch"),
        attended,
        residual[0],
        norm_gain.reshape(1, -1),
        span_lengths,
        positives.reshape(1, -1),
        out_weight,
        source_queue,
        own_rows,
    )
    return (anchors[None], losses[:, 0][None])


def solution(mesh):
    return jax.shard_map(
        body,
        mesh=mesh,
        in_specs=(
            P("batch", "seq", None),
            P("batch", "seq", None),
            P("batch", "seq", None),
            P("batch", "seq", None),
            P(),
            P(),
            P("batch", None),
            P("batch", None),
            P(None, "seq"),
        ),
        out_specs=(P("batch", "seq", None), P("batch", "seq")),
        check_vma=False,
    )
```

```python
import functools
import math

import jax
import jax.numpy as jnp
from jax import lax
from jax.experimental import pallas as pl
from jax.experimental.pallas import tpu as pltpu
from jax.sharding import PartitionSpec as P

HEADS = 16
WINDOW = 512
MESH = pl.DeviceIdType.MESH
F32 = jnp.float32
BF16 = jnp.bfloat16


logit_scale = 20.0


NEVER = -1e30


def scores_to_partial(query_chunk, key_chunk, value_t, blocks_apart, head_size):
    tok_rows, width = query_chunk.shape
    lane = lax.broadcasted_iota(jnp.int32, (tok_rows, width), 1)
    key_at = lax.broadcasted_iota(jnp.int32, (tok_rows, tok_rows), 0)
    query_at = lax.broadcasted_iota(jnp.int32, (tok_rows, tok_rows), 1)
    distance = blocks_apart * tok_rows + query_at - key_at
    low = blocks_apart * tok_rows - (tok_rows - 1)
    high = blocks_apart * tok_rows + tok_rows - 1
    mixed, peaks, totals = [], [], []
    for h in range(width // head_size):
        own = (lane >= h * head_size) & (lane < (h + 1) * head_size)
        query_h = jnp.where(own, query_chunk, jnp.zeros_like(query_chunk))
        scores = lax.dot_general(
            key_chunk, query_h, (((1,), (1,)), ((), ())), preferred_element_type=F32
        ) * (1.0 / math.sqrt(head_size))
        if low < 0:
            scores = jnp.where(distance >= 0, scores, NEVER)
        if high >= WINDOW:
            scores = jnp.where(distance < WINDOW, scores, NEVER)
        peak = jnp.max(scores, axis=0, keepdims=True)
        weights = jnp.exp(scores - peak)
        totals.append(jnp.sum(weights, axis=0, keepdims=True))
        peaks.append(peak)
        mixed.append(
            jnp.dot(
                value_t[h * head_size : (h + 1) * head_size, :],
                weights.astype(BF16),
                preferred_element_type=F32,
            )
        )
    stats = jnp.concatenate(
        peaks + totals + [jnp.zeros((8 - 2 * len(peaks), tok_rows), F32)], axis=0
    )
    return jnp.concatenate(mixed, axis=0), stats


def merged(mixed_a, stats_a, mixed_b, stats_b, heads, head_size):
    mixed, peaks, totals = [], [], []
    for h in range(heads):
        rows = slice(h * head_size, (h + 1) * head_size)
        peak_a, peak_b = stats_a[h : h + 1], stats_b[h : h + 1]
        peak = jnp.maximum(peak_a, peak_b)
        keep_a, keep_b = jnp.exp(peak_a - peak), jnp.exp(peak_b - peak)
        mixed.append(mixed_a[rows].astype(F32) * keep_a + mixed_b[rows].astype(F32) * keep_b)
        totals.append(
            stats_a[heads + h : heads + h + 1] * keep_a
            + stats_b[heads + h : heads + h + 1] * keep_b
        )
        peaks.append(peak)
    return mixed, peaks, totals


def block_kernel(
    n_seq,
    n_batch,
    head_size,
    gain_ref,
    lengths_ref,
    wanted_ref,
    queries_hbm,
    keys_hbm,
    values_hbm,
    residual_hbm,
    weight_hbm,
    queue_hbm,
    anchors_ref,
    losses_ref,
    q_own,
    k_own,
    v_own,
    v_t,
    q_one,
    q_two,
    mix_own,
    stat_own,
    mix_one,
    stat_one,
    two_out,
    two_out_stat,
    two_in,
    two_in_stat,
    one_out,
    one_out_stat,
    one_in,
    one_in_stat,
    att_t,
    residual,
    weight,
    queue,
    parts,
    parts_in,
    anchors_all,
    stats,
    chunk_sem,
    load_sem,
    send_sem,
    recv_sem,
    part_send,
    part_recv,
    anchor_send,
    anchor_recv,
    stat_send,
    stat_recv,
):
    chunks, tok_rows, chunk_cols = q_own.shape
    heads = chunk_cols // head_size
    own_rows, width = anchors_ref.shape
    funcs = own_rows * n_seq
    seq = lax.axis_index("seq")
    batch = lax.axis_index("batch")

    def load(which, g):
        source = (queries_hbm, keys_hbm, values_hbm)[which]
        target = (q_own, k_own, v_own)[which]
        cols = pl.ds(pl.multiple_of(g * chunk_cols, chunk_cols), chunk_cols)
        return pltpu.make_async_copy(
            source.at[:, cols], target.at[g], chunk_sem.at[which, g]
        )

    def start_loads(g, carry):
        for which in range(3):
            load(which, g).start()
        return carry

    lax.fori_loop(0, chunks, start_loads, 0)
    residual_load = pltpu.make_async_copy(residual_hbm, residual, load_sem.at[0])
    weight_load = pltpu.make_async_copy(weight_hbm, weight, load_sem.at[1])
    queue_load = pltpu.make_async_copy(queue_hbm, queue, load_sem.at[2])
    residual_load.start()
    weight_load.start()
    queue_load.start()

    seq_peers = [lax.rem(seq + d, n_seq) for d in range(1, n_seq)]
    batch_peers = [lax.rem(batch + d, n_batch) for d in range(1, n_batch)]
    barrier = pltpu.get_barrier_semaphore()
    for peer in seq_peers:
        pl.semaphore_signal(barrier, inc=1, device_id={"seq": peer}, device_id_type=MESH)
    for peer in batch_peers:
        pl.semaphore_signal(barrier, inc=1, device_id={"batch": peer}, device_id_type=MESH)
    pl.semaphore_wait(barrier, n_seq - 1 + n_batch - 1)

    left = lax.rem(seq + n_seq - 1, n_seq)
    right = lax.rem(seq + 1, n_seq)
    has_left = seq >= 1
    has_right = seq <= n_seq - 2
    has_right_two = seq <= n_seq - 3

    def remote(kind, source, target, g, peer):
        return pltpu.make_async_remote_copy(
            src_ref=source.at[g],
            dst_ref=target.at[g],
            send_sem=send_sem.at[kind, g],
            recv_sem=recv_sem.at[kind, g],
            device_id={"seq": peer},
            device_id_type=MESH,
        )

    def ask_one(g):
        return remote(0, q_own, q_one, g, left)

    def ask_two(g):
        return remote(1, q_one, q_two, g, left)

    def give_two(g):
        return (
            remote(2, two_out, two_in, g, right),
            remote(3, two_out_stat, two_in_stat, g, right),
        )

    def give_one(g):
        return (
            remote(4, one_out, one_in, g, right),
            remote(5, one_out_stat, one_in_stat, g, right),
        )

    ahead = min(3, chunks)
    for g in range(ahead):
        load(0, g).wait()

        @pl.when(has_left)
        def _():
            ask_one(g).start()

    def step(t, carry):
        fresh = t < chunks

        @pl.when(fresh & has_right)
        def _():
            ask_one(t).wait_recv()

            @pl.when(has_left)
            def _():
                ask_two(t).start()

        @pl.when(t + ahead < chunks)
        def _():
            load(0, t + ahead).wait()

            @pl.when(has_left)
            def _():
                ask_one(t + ahead).start()

        @pl.when(fresh)
        def _():
            load(1, t).wait()
            load(2, t).wait()
            v_t[t] = v_own[t].T

        @pl.when((t >= 2) & (t < chunks + 2) & has_right_two)
        def _():
            g = t - 2
            ask_two(g).wait_recv()
            mixed, stat = scores_to_partial(q_two[g], k_own[g], v_t.at[g], 2, head_size)
            two_out[g] = mixed.astype(BF16)
            two_out_stat[g] = stat
            for copy in give_two(g):
                copy.start()

        @pl.when((t >= 4) & (t < chunks + 4) & has_right)
        def _():
            g = t - 4

            @pl.when(has_left)
            def _():
                for copy in give_two(g):
                    copy.wait_recv()
                mixed, peaks, totals = merged(
                    mix_one[g], stat_one[g], two_in[g], two_in_stat[g], heads, head_size
                )
                one_out[g] = jnp.concatenate(mixed, axis=0).astype(BF16)
                one_out_stat[g] = jnp.concatenate(
                    peaks + totals + [jnp.zeros((8 - 2 * heads, tok_rows), F32)], axis=0
                )

            @pl.when(jnp.logical_not(has_left))
            def _():
                one_out[g] = mix_one[g].astype(BF16)
                one_out_stat[g] = stat_one[g]

            for copy in give_one(g):
                copy.start()

        @pl.when(fresh)
        def _():
            mixed, stat = scores_to_partial(q_own[t], k_own[t], v_t.at[t], 0, head_size)
            mix_own[t] = mixed
            stat_own[t] = stat

        @pl.when(fresh & has_right)
        def _():
            mixed, stat = scores_to_partial(q_one[t], k_own[t], v_t.at[t], 1, head_size)
            mix_one[t] = mixed
            stat_one[t] = stat

        @pl.when((t >= 6) & (t < chunks + 6))
        def _():
            g = t - 6

            @pl.when(has_left)
            def _():
                for copy in give_one(g):
                    copy.wait_recv()
                mixed, peaks, totals = merged(
                    mix_own[g], stat_own[g], one_in[g], one_in_stat[g], heads, head_size
                )
                att_t[g] = jnp.concatenate(
                    [m / l for m, l in zip(mixed, totals)], axis=0
                ).astype(BF16)

            @pl.when(jnp.logical_not(has_left))
            def _():
                for h in range(heads):
                    rows = slice(h * head_size, (h + 1) * head_size)
                    att_t[g, rows, :] = (
                        mix_own[g, rows, :] / stat_own[g, heads + h : heads + h + 1, :]
                    ).astype(BF16)

        return carry

    lax.fori_loop(0, chunks + 6, step, 0)

    residual_load.wait()
    weight_load.wait()
    hidden = residual[...].astype(F32) + lax.dot_general(
        att_t[...].reshape(width, tok_rows),
        weight[...],
        (((0,), (0,)), ((), ())),
        preferred_element_type=F32,
    )
    scale = lax.rsqrt(jnp.mean(hidden * hidden, axis=-1, keepdims=True) + 1e-05)
    normed = (hidden * scale * gain_ref[...]).astype(BF16)

    row_ids = lax.broadcasted_iota(jnp.int32, (funcs, funcs), 0)
    func_ids = lax.broadcasted_iota(jnp.int32, (funcs, funcs), 1)
    listed = lax.rem(row_ids, own_rows) * n_seq + row_ids // own_rows
    lengths = jnp.broadcast_to(lengths_ref[...].astype(F32), (funcs, funcs))
    begin_at = jnp.sum(jnp.where(func_ids < listed, lengths, 0.0), axis=1, keepdims=True)
    end_at = jnp.sum(jnp.where(func_ids <= listed, lengths, 0.0), axis=1, keepdims=True)
    pos = (
        seq * tok_rows + lax.broadcasted_iota(jnp.int32, (funcs, tok_rows), 1)
    ).astype(F32)
    member = jnp.where((pos >= begin_at) & (pos < end_at), 1.0, 0.0).astype(BF16)
    partial = jnp.dot(member, normed, preferred_element_type=F32)
    parts[...] = partial.reshape(n_seq, own_rows, width).astype(BF16)

    copies = []
    for d in range(1, n_seq):
        copy = pltpu.make_async_remote_copy(
            src_ref=parts.at[seq_peers[d - 1]],
            dst_ref=parts_in.at[d - 1],
            send_sem=part_send.at[d - 1],
            recv_sem=part_recv.at[d - 1],
            device_id={"seq": seq_peers[d - 1]},
            device_id_type=MESH,
        )
        copy.start()
        copies.append(copy)
    pooled = parts[seq].astype(F32)
    for d in range(1, n_seq):
        copies[d - 1].wait_recv()
        pooled = pooled + parts_in[d - 1].astype(F32)
    anchors = (
        pooled * lax.rsqrt(jnp.sum(pooled * pooled, axis=-1, keepdims=True) + 1e-06)
    ).astype(BF16)
    anchors_ref[...] = anchors
    anchors_all[batch] = anchors
    for copy in copies:
        copy.wait_send()

    copies = []
    for d in range(1, n_batch):
        copy = pltpu.make_async_remote_copy(
            src_ref=anchors_all.at[batch],
            dst_ref=anchors_all.at[batch],
            send_sem=anchor_send.at[d - 1],
            recv_sem=anchor_recv.at[d - 1],
            device_id={"batch": batch_peers[d - 1]},
            device_id_type=MESH,
        )
        copy.start()
        copies.append(copy)
    queue_load.wait()
    for copy in copies:
        copy.wait()
    rows = n_batch * own_rows
    logits = logit_scale * lax.dot_general(
        queue[...],
        anchors_all[...].reshape(rows, width),
        (((1,), (1,)), ((), ())),
        preferred_element_type=F32,
    )
    queue_rows = queue.shape[0]
    queue_ids = batch * queue_rows + lax.broadcasted_iota(jnp.int32, logits.shape, 0)
    row_peak = jnp.max(logits, axis=0, keepdims=True)
    row_total = jnp.sum(jnp.exp(logits - row_peak), axis=0, keepdims=True)
    positive = jnp.sum(
        jnp.where(wanted_ref[...] == queue_ids, logits, 0.0), axis=0, keepdims=True
    )
    stats[batch] = jnp.concatenate(
        [row_peak, row_total, positive, jnp.zeros((5, rows), F32)], axis=0
    )
    copies = []
    for d in range(1, n_batch):
        copy = pltpu.make_async_remote_copy(
            src_ref=stats.at[batch],
            dst_ref=stats.at[batch],
            send_sem=stat_send.at[d - 1],
            recv_sem=stat_recv.at[d - 1],
            device_id={"batch": batch_peers[d - 1]},
            device_id_type=MESH,
        )
        copy.start()
        copies.append(copy)
    for copy in copies:
        copy.wait()
    peaks = [stats[b, 0:1, :] for b in range(n_batch)]
    top = functools.reduce(jnp.maximum, peaks)
    total = sum(stats[b, 1:2, :] * jnp.exp(peaks[b] - top) for b in range(n_batch))
    chosen = sum(stats[b, 2:3, :] for b in range(n_batch))
    loss = top + jnp.log(total) - chosen
    loss_col = jnp.sum(
        jnp.where(
            lax.broadcasted_iota(jnp.int32, (own_rows, rows), 1)
            == batch * own_rows + lax.broadcasted_iota(jnp.int32, (own_rows, rows), 0),
            jnp.broadcast_to(loss, (own_rows, rows)),
            0.0,
        ),
        axis=1,
        keepdims=True,
    )
    losses_ref[...] = jnp.broadcast_to(loss_col, losses_ref.shape)

    def drain(g, carry):
        @pl.when(has_left)
        def _():
            ask_one(g).wait_send()

            @pl.when(has_right)
            def _():
                ask_two(g).wait_send()

        @pl.when(has_right_two)
        def _():
            for copy in give_two(g):
                copy.wait_send()

        @pl.when(has_right)
        def _():
            for copy in give_one(g):
                copy.wait_send()

        return carry

    lax.fori_loop(0, chunks, drain, 0)


def body(
    queries, keys, values, residual, out_weight, norm_gain, source_queue, span_lengths, positives
):
    tok_rows, width = queries.shape[1:]
    head_size = width // HEADS
    n_seq = lax.axis_size("seq")
    n_batch = lax.axis_size("batch")
    own_rows = positives.shape[1]
    rows = n_batch * own_rows
    chunk_cols = 128
    chunks = width // chunk_cols
    assert (WINDOW - 1) // tok_rows + 1 == 2 and chunk_cols % head_size == 0
    vmem = pl.BlockSpec(memory_space=pltpu.VMEM)
    hbm = pl.BlockSpec(memory_space=pl.ANY)
    rows_bf16 = pltpu.VMEM((chunks, tok_rows, chunk_cols), BF16)
    cols_bf16 = pltpu.VMEM((chunks, chunk_cols, tok_rows), BF16)
    cols_f32 = pltpu.VMEM((chunks, chunk_cols, tok_rows), F32)
    stat_f32 = pltpu.VMEM((chunks, 8, tok_rows), F32)
    anchors, losses = pl.pallas_call(
        functools.partial(block_kernel, n_seq, n_batch, head_size),
        out_shape=(
            jax.ShapeDtypeStruct((own_rows, width), BF16),
            jax.ShapeDtypeStruct((own_rows, 128), F32),
        ),
        in_specs=[vmem] * 3 + [hbm] * 6,
        out_specs=(vmem, vmem),
        scratch_shapes=[
            rows_bf16,
            rows_bf16,
            rows_bf16,
            cols_bf16,
            rows_bf16,
            rows_bf16,
            cols_f32,
            stat_f32,
            cols_f32,
            stat_f32,
            cols_bf16,
            stat_f32,
            cols_bf16,
            stat_f32,
            cols_bf16,
            stat_f32,
            cols_bf16,
            stat_f32,
            cols_bf16,
            pltpu.VMEM((tok_rows, width), BF16),
            pltpu.VMEM(out_weight.shape, BF16),
            pltpu.VMEM(source_queue.shape, BF16),
            pltpu.VMEM((n_seq, own_rows, width), BF16),
            pltpu.VMEM((n_seq - 1, own_rows, width), BF16),
            pltpu.VMEM((n_batch, own_rows, width), BF16),
            pltpu.VMEM((n_batch, 8, rows), F32),
            pltpu.SemaphoreType.DMA((3, chunks)),
            pltpu.SemaphoreType.DMA((3,)),
            pltpu.SemaphoreType.DMA((6, chunks)),
            pltpu.SemaphoreType.DMA((6, chunks)),
            pltpu.SemaphoreType.DMA((n_seq - 1,)),
            pltpu.SemaphoreType.DMA((n_seq - 1,)),
            pltpu.SemaphoreType.DMA((n_batch - 1,)),
            pltpu.SemaphoreType.DMA((n_batch - 1,)),
            pltpu.SemaphoreType.DMA((n_batch - 1,)),
            pltpu.SemaphoreType.DMA((n_batch - 1,)),
        ],
        compiler_params=pltpu.CompilerParams(
            collective_id=0, has_side_effects=True, vmem_limit_bytes=48 * 1024 * 1024
        ),
        name="block",
    )(
        norm_gain.reshape(1, -1),
        span_lengths,
        positives.reshape(1, -1),
        queries[0],
        keys[0],
        values[0],
        residual[0],
        out_weight,
        source_queue,
    )
    return (anchors[None], losses[:, 0][None])


def solution(mesh):
    return jax.shard_map(
        body,
        mesh=mesh,
        in_specs=(
            P("batch", "seq", None),
            P("batch", "seq", None),
            P("batch", "seq", None),
            P("batch", "seq", None),
            P(),
            P(),
            P("batch", None),
            P("batch", None),
            P(None, "seq"),
        ),
        out_specs=(P("batch", "seq", None), P("batch", "seq")),
        check_vma=False,
    )
```

```python
import functools
import math

import jax
import jax.numpy as jnp
from jax import lax
from jax.experimental import pallas as pl
from jax.experimental.pallas import tpu as pltpu
from jax.sharding import PartitionSpec as P

HEADS = 16
WINDOW = 512
MESH = pl.DeviceIdType.MESH
F32 = jnp.float32
BF16 = jnp.bfloat16


logit_scale = 20.0


NEVER = -1e30


def scores_to_partial(query_chunk, key_ref, value_t, blocks_apart, head_size):
    tok_rows, width = query_chunk.shape
    half = tok_rows // 2
    to_log2 = math.log2(math.e) / math.sqrt(head_size)
    lane = lax.broadcasted_iota(jnp.int32, (tok_rows, width), 1)
    query_less_key = lax.broadcasted_iota(jnp.int32, (half, half), 1) - lax.broadcasted_iota(
        jnp.int32, (half, half), 0
    )
    mixed, peaks, totals = [], [], []
    for h in range(width // head_size):
        own = (lane >= h * head_size) & (lane < (h + 1) * head_size)
        query_h = jnp.where(own, query_chunk, jnp.zeros_like(query_chunk))
        mixed_h, peaks_h, totals_h = [], [], []
        for i in range(2):
            offsets = [blocks_apart * tok_rows + (i - j) * half for j in range(2)]
            seen = [j for j in range(2) if -half < offsets[j] < WINDOW + half - 1]
            first, last = seen[0] * half, (seen[-1] + 1) * half
            scores = lax.dot_general(
                key_ref[first:last, :],
                query_h[i * half : (i + 1) * half],
                (((1,), (1,)), ((), ())),
                preferred_element_type=F32,
            )
            parts = []
            for j in seen:
                part = scores[j * half - first : (j + 1) * half - first]
                if offsets[j] < half - 1:
                    part = jnp.where(query_less_key >= -offsets[j], part, NEVER)
                if offsets[j] + half - 1 >= WINDOW:
                    part = jnp.where(query_less_key < WINDOW - offsets[j], part, NEVER)
                parts.append(part)
            peak = functools.reduce(
                jnp.maximum, [jnp.max(part, axis=0, keepdims=True) for part in parts]
            )
            parts = [jnp.exp2((part - peak) * to_log2) for part in parts]
            totals_h.append(sum(jnp.sum(part, axis=0, keepdims=True) for part in parts))
            peaks_h.append(peak)
            mixed_h.append(
                jnp.dot(
                    value_t[h * head_size : (h + 1) * head_size, first:last],
                    jnp.concatenate([part.astype(BF16) for part in parts], axis=0),
                    preferred_element_type=F32,
                )
            )
        mixed.append(jnp.concatenate(mixed_h, axis=1))
        peaks.append(jnp.concatenate(peaks_h, axis=1))
        totals.append(jnp.concatenate(totals_h, axis=1))
    stats = jnp.concatenate(
        peaks + totals + [jnp.zeros((8 - 2 * len(peaks), tok_rows), F32)], axis=0
    )
    return jnp.concatenate(mixed, axis=0), stats


def merged(mixed_a, stats_a, mixed_b, stats_b, heads, head_size):
    to_log2 = math.log2(math.e) / math.sqrt(head_size)
    mixed, peaks, totals = [], [], []
    for h in range(heads):
        rows = slice(h * head_size, (h + 1) * head_size)
        peak_a, peak_b = stats_a[h : h + 1], stats_b[h : h + 1]
        peak = jnp.maximum(peak_a, peak_b)
        keep_a = jnp.exp2((peak_a - peak) * to_log2)
        keep_b = jnp.exp2((peak_b - peak) * to_log2)
        mixed.append(mixed_a[rows].astype(F32) * keep_a + mixed_b[rows].astype(F32) * keep_b)
        totals.append(
            stats_a[heads + h : heads + h + 1] * keep_a
            + stats_b[heads + h : heads + h + 1] * keep_b
        )
        peaks.append(peak)
    return mixed, peaks, totals


def block_kernel(
    n_seq,
    n_batch,
    head_size,
    gain_ref,
    lengths_ref,
    wanted_ref,
    queries_hbm,
    keys_hbm,
    values_hbm,
    residual_hbm,
    weight_hbm,
    queue_hbm,
    anchors_ref,
    losses_ref,
    q_own,
    k_own,
    v_own,
    v_t,
    q_one,
    q_two,
    mix_own,
    stat_own,
    mix_one,
    stat_one,
    two_out,
    two_out_stat,
    two_in,
    two_in_stat,
    one_out,
    one_out_stat,
    one_in,
    one_in_stat,
    att_t,
    residual,
    weight,
    queue,
    parts,
    parts_in,
    anchors_all,
    stats,
    wanted,
    chunk_sem,
    load_sem,
    send_sem,
    recv_sem,
    part_send,
    part_recv,
    anchor_send,
    anchor_recv,
    stat_send,
    stat_recv,
):
    chunks, tok_rows, chunk_cols = q_own.shape
    heads = chunk_cols // head_size
    own_rows, width = anchors_ref.shape
    funcs = own_rows * n_seq
    seq = lax.axis_index("seq")
    batch = lax.axis_index("batch")

    def load(which, g):
        source = (queries_hbm, keys_hbm, values_hbm)[which]
        target = (q_own, k_own, v_own)[which]
        cols = pl.ds(pl.multiple_of(g * chunk_cols, chunk_cols), chunk_cols)
        return pltpu.make_async_copy(
            source.at[:, cols], target.at[g], chunk_sem.at[which, g]
        )

    def start_loads(g, carry):
        for which in range(3):
            load(which, g).start()
        return carry

    lax.fori_loop(0, chunks, start_loads, 0)
    residual_load = pltpu.make_async_copy(residual_hbm, residual, load_sem.at[0])
    weight_load = pltpu.make_async_copy(weight_hbm, weight, load_sem.at[1])
    queue_load = pltpu.make_async_copy(queue_hbm, queue, load_sem.at[2])
    residual_load.start()
    weight_load.start()
    queue_load.start()

    rows = n_batch * own_rows
    spread_at = lax.broadcasted_iota(jnp.int32, (own_rows, rows), 1)
    spread = (
        lax.rem(spread_at, own_rows) == lax.broadcasted_iota(jnp.int32, (own_rows, rows), 0)
    )
    spread = jnp.where(spread, 1.0, 0.0).astype(BF16)
    high = wanted_ref[...] // 128
    low = wanted_ref[...] - high * 128
    whole = 128.0 * jnp.dot(
        high.astype(F32).astype(BF16), spread, preferred_element_type=F32
    ) + jnp.dot(low.astype(F32).astype(BF16), spread, preferred_element_type=F32)
    mine = lax.broadcasted_iota(jnp.int32, (n_batch, rows), 1) // own_rows
    mine = mine == lax.broadcasted_iota(jnp.int32, (n_batch, rows), 0)
    wanted[...] = jnp.sum(jnp.where(mine, whole, 0.0), axis=0, keepdims=True).astype(jnp.int32)

    seq_peers = [lax.rem(seq + d, n_seq) for d in range(1, n_seq)]
    batch_peers = [lax.rem(batch + d, n_batch) for d in range(1, n_batch)]
    barrier = pltpu.get_barrier_semaphore()
    for peer in seq_peers:
        pl.semaphore_signal(barrier, inc=1, device_id={"seq": peer}, device_id_type=MESH)
    for peer in batch_peers:
        pl.semaphore_signal(barrier, inc=1, device_id={"batch": peer}, device_id_type=MESH)
    pl.semaphore_wait(barrier, n_seq - 1 + n_batch - 1)

    left = lax.rem(seq + n_seq - 1, n_seq)
    right = lax.rem(seq + 1, n_seq)
    has_left = seq >= 1
    has_right = seq <= n_seq - 2
    has_right_two = seq <= n_seq - 3

    def remote(kind, source, target, g, peer):
        return pltpu.make_async_remote_copy(
            src_ref=source.at[g],
            dst_ref=target.at[g],
            send_sem=send_sem.at[kind, g],
            recv_sem=recv_sem.at[kind, g],
            device_id={"seq": peer},
            device_id_type=MESH,
        )

    def ask_one(g):
        return remote(0, q_own, q_one, g, left)

    def ask_two(g):
        return remote(1, q_one, q_two, g, left)

    def give_two(g):
        return (
            remote(2, two_out, two_in, g, right),
            remote(3, two_out_stat, two_in_stat, g, right),
        )

    def give_one(g):
        return (
            remote(4, one_out, one_in, g, right),
            remote(5, one_out_stat, one_in_stat, g, right),
        )

    ahead = min(3, chunks)
    for g in range(ahead):
        load(0, g).wait()

        @pl.when(has_left)
        def _():
            ask_one(g).start()

    def attend_own(g):
        load(1, g).wait()
        load(2, g).wait()
        v_t[g] = v_own[g].T
        mixed, stat = scores_to_partial(q_own[g], k_own.at[g], v_t.at[g], 0, head_size)
        mix_own[g] = mixed
        stat_own[g] = stat

    def attend_first(g, carry):
        attend_own(g)
        return carry

    lax.fori_loop(0, ahead, attend_first, 0)

    def step(t, carry):
        fresh = t < chunks

        @pl.when(fresh & has_right)
        def _():
            ask_one(t).wait_recv()

            @pl.when(has_left)
            def _():
                ask_two(t).start()

        @pl.when(t + ahead < chunks)
        def _():
            load(0, t + ahead).wait()

            @pl.when(has_left)
            def _():
                ask_one(t + ahead).start()

        @pl.when((t >= 2) & (t < chunks + 2) & has_right_two)
        def _():
            g = t - 2
            ask_two(g).wait_recv()
            mixed, stat = scores_to_partial(q_two[g], k_own.at[g], v_t.at[g], 2, head_size)
            two_out[g] = mixed.astype(BF16)
            two_out_stat[g] = stat
            for copy in give_two(g):
                copy.start()

        @pl.when((t >= 4) & (t < chunks + 4) & has_right)
        def _():
            g = t - 4

            @pl.when(has_left)
            def _():
                for copy in give_two(g):
                    copy.wait_recv()
                mixed, peaks, totals = merged(
                    mix_one[g], stat_one[g], two_in[g], two_in_stat[g], heads, head_size
                )
                one_out[g] = jnp.concatenate(mixed, axis=0).astype(BF16)
                one_out_stat[g] = jnp.concatenate(
                    peaks + totals + [jnp.zeros((8 - 2 * heads, tok_rows), F32)], axis=0
                )

            @pl.when(jnp.logical_not(has_left))
            def _():
                one_out[g] = mix_one[g].astype(BF16)
                one_out_stat[g] = stat_one[g]

            for copy in give_one(g):
                copy.start()

        @pl.when(fresh & has_right)
        def _():
            mixed, stat = scores_to_partial(q_one[t], k_own.at[t], v_t.at[t], 1, head_size)
            mix_one[t] = mixed
            stat_one[t] = stat

        @pl.when(t + ahead < chunks)
        def _():
            attend_own(t + ahead)

        @pl.when((t >= 6) & (t < chunks + 6))
        def _():
            g = t - 6

            @pl.when(has_left)
            def _():
                for copy in give_one(g):
                    copy.wait_recv()
                mixed, peaks, totals = merged(
                    mix_own[g], stat_own[g], one_in[g], one_in_stat[g], heads, head_size
                )
                att_t[g] = jnp.concatenate(
                    [m / l for m, l in zip(mixed, totals)], axis=0
                ).astype(BF16)

            @pl.when(jnp.logical_not(has_left))
            def _():
                for h in range(heads):
                    rows = slice(h * head_size, (h + 1) * head_size)
                    att_t[g, rows, :] = (
                        mix_own[g, rows, :] / stat_own[g, heads + h : heads + h + 1, :]
                    ).astype(BF16)

        return carry

    lax.fori_loop(0, chunks + 6, step, 0)

    residual_load.wait()
    weight_load.wait()
    hidden = residual[...].astype(F32) + lax.dot_general(
        att_t[...].reshape(width, tok_rows),
        weight[...],
        (((0,), (0,)), ((), ())),
        preferred_element_type=F32,
    )
    scale = lax.rsqrt(jnp.mean(hidden * hidden, axis=-1, keepdims=True) + 1e-05)
    normed = (hidden * scale * gain_ref[...]).astype(BF16)

    row_ids = lax.broadcasted_iota(jnp.int32, (funcs, funcs), 0)
    func_ids = lax.broadcasted_iota(jnp.int32, (funcs, funcs), 1)
    listed = lax.rem(row_ids, own_rows) * n_seq + row_ids // own_rows
    lengths = jnp.broadcast_to(lengths_ref[...].astype(F32), (funcs, funcs))
    begin_at = jnp.sum(jnp.where(func_ids < listed, lengths, 0.0), axis=1, keepdims=True)
    end_at = jnp.sum(jnp.where(func_ids <= listed, lengths, 0.0), axis=1, keepdims=True)
    pos = (
        seq * tok_rows + lax.broadcasted_iota(jnp.int32, (funcs, tok_rows), 1)
    ).astype(F32)
    member = jnp.where((pos >= begin_at) & (pos < end_at), 1.0, 0.0).astype(BF16)
    partial = jnp.dot(member, normed, preferred_element_type=F32)
    parts[...] = partial.reshape(n_seq, own_rows, width).astype(BF16)

    copies = []
    for d in range(1, n_seq):
        copy = pltpu.make_async_remote_copy(
            src_ref=parts.at[seq_peers[d - 1]],
            dst_ref=parts_in.at[d - 1],
            send_sem=part_send.at[d - 1],
            recv_sem=part_recv.at[d - 1],
            device_id={"seq": seq_peers[d - 1]},
            device_id_type=MESH,
        )
        copy.start()
        copies.append(copy)
    pooled = parts[seq].astype(F32)
    for d in range(1, n_seq):
        copies[d - 1].wait_recv()
        pooled = pooled + parts_in[d - 1].astype(F32)
    anchors = (
        pooled * lax.rsqrt(jnp.sum(pooled * pooled, axis=-1, keepdims=True) + 1e-06)
    ).astype(BF16)
    anchors_ref[...] = anchors
    anchors_all[batch] = anchors
    for copy in copies:
        copy.wait_send()

    copies = []
    for d in range(1, n_batch):
        copy = pltpu.make_async_remote_copy(
            src_ref=anchors_all.at[batch],
            dst_ref=anchors_all.at[batch],
            send_sem=anchor_send.at[d - 1],
            recv_sem=anchor_recv.at[d - 1],
            device_id={"batch": batch_peers[d - 1]},
            device_id_type=MESH,
        )
        copy.start()
        copies.append(copy)
    queue_load.wait()
    for copy in copies:
        copy.wait()
    logits = logit_scale * lax.dot_general(
        queue[...],
        anchors_all[...].reshape(rows, width),
        (((1,), (1,)), ((), ())),
        preferred_element_type=F32,
    )
    queue_rows = queue.shape[0]
    queue_ids = batch * queue_rows + lax.broadcasted_iota(jnp.int32, logits.shape, 0)
    row_peak = jnp.max(logits, axis=0, keepdims=True)
    row_total = jnp.sum(jnp.exp(logits - row_peak), axis=0, keepdims=True)
    positive = jnp.sum(
        jnp.where(wanted[...] == queue_ids, logits, 0.0), axis=0, keepdims=True
    )
    stats[batch] = jnp.concatenate(
        [row_peak, row_total, positive, jnp.zeros((5, rows), F32)], axis=0
    )
    copies = []
    for d in range(1, n_batch):
        copy = pltpu.make_async_remote_copy(
            src_ref=stats.at[batch],
            dst_ref=stats.at[batch],
            send_sem=stat_send.at[d - 1],
            recv_sem=stat_recv.at[d - 1],
            device_id={"batch": batch_peers[d - 1]},
            device_id_type=MESH,
        )
        copy.start()
        copies.append(copy)
    for copy in copies:
        copy.wait()
    peaks = [stats[b, 0:1, :] for b in range(n_batch)]
    top = functools.reduce(jnp.maximum, peaks)
    total = sum(stats[b, 1:2, :] * jnp.exp(peaks[b] - top) for b in range(n_batch))
    chosen = sum(stats[b, 2:3, :] for b in range(n_batch))
    loss = top + jnp.log(total) - chosen
    loss_col = jnp.sum(
        jnp.where(
            lax.broadcasted_iota(jnp.int32, (own_rows, rows), 1)
            == batch * own_rows + lax.broadcasted_iota(jnp.int32, (own_rows, rows), 0),
            jnp.broadcast_to(loss, (own_rows, rows)),
            0.0,
        ),
        axis=1,
        keepdims=True,
    )
    square = (own_rows, own_rows)
    diagonal = lax.broadcasted_iota(jnp.int32, square, 0) == lax.broadcasted_iota(
        jnp.int32, square, 1
    )
    losses_ref[...] = jnp.sum(
        jnp.where(diagonal, jnp.broadcast_to(loss_col, square), 0.0), axis=0, keepdims=True
    )

    def drain(g, carry):
        @pl.when(has_left)
        def _():
            ask_one(g).wait_send()

            @pl.when(has_right)
            def _():
                ask_two(g).wait_send()

        @pl.when(has_right_two)
        def _():
            for copy in give_two(g):
                copy.wait_send()

        @pl.when(has_right)
        def _():
            for copy in give_one(g):
                copy.wait_send()

        return carry

    lax.fori_loop(0, chunks, drain, 0)


def body(
    queries, keys, values, residual, out_weight, norm_gain, source_queue, span_lengths, positives
):
    tok_rows, width = queries.shape[1:]
    head_size = width // HEADS
    n_seq = lax.axis_size("seq")
    n_batch = lax.axis_size("batch")
    own_rows = positives.shape[1]
    rows = n_batch * own_rows
    chunk_cols = 128
    chunks = width // chunk_cols
    assert (WINDOW - 1) // tok_rows + 1 == 2 and chunk_cols % head_size == 0
    vmem = pl.BlockSpec(memory_space=pltpu.VMEM)
    hbm = pl.BlockSpec(memory_space=pl.ANY)
    rows_bf16 = pltpu.VMEM((chunks, tok_rows, chunk_cols), BF16)
    cols_bf16 = pltpu.VMEM((chunks, chunk_cols, tok_rows), BF16)
    cols_f32 = pltpu.VMEM((chunks, chunk_cols, tok_rows), F32)
    stat_f32 = pltpu.VMEM((chunks, 8, tok_rows), F32)
    anchors, losses = pl.pallas_call(
        functools.partial(block_kernel, n_seq, n_batch, head_size),
        out_shape=(
            jax.ShapeDtypeStruct((own_rows, width), BF16),
            jax.ShapeDtypeStruct((1, own_rows), F32),
        ),
        in_specs=[vmem] * 3 + [hbm] * 6,
        out_specs=(vmem, vmem),
        scratch_shapes=[
            rows_bf16,
            rows_bf16,
            rows_bf16,
            cols_bf16,
            rows_bf16,
            rows_bf16,
            cols_f32,
            stat_f32,
            cols_f32,
            stat_f32,
            cols_bf16,
            stat_f32,
            cols_bf16,
            stat_f32,
            cols_bf16,
            stat_f32,
            cols_bf16,
            stat_f32,
            cols_bf16,
            pltpu.VMEM((tok_rows, width), BF16),
            pltpu.VMEM(out_weight.shape, BF16),
            pltpu.VMEM(source_queue.shape, BF16),
            pltpu.VMEM((n_seq, own_rows, width), BF16),
            pltpu.VMEM((n_seq - 1, own_rows, width), BF16),
            pltpu.VMEM((n_batch, own_rows, width), BF16),
            pltpu.VMEM((n_batch, 8, rows), F32),
            pltpu.VMEM((1, rows), jnp.int32),
            pltpu.SemaphoreType.DMA((3, chunks)),
            pltpu.SemaphoreType.DMA((3,)),
            pltpu.SemaphoreType.DMA((6, chunks)),
            pltpu.SemaphoreType.DMA((6, chunks)),
            pltpu.SemaphoreType.DMA((n_seq - 1,)),
            pltpu.SemaphoreType.DMA((n_seq - 1,)),
            pltpu.SemaphoreType.DMA((n_batch - 1,)),
            pltpu.SemaphoreType.DMA((n_batch - 1,)),
            pltpu.SemaphoreType.DMA((n_batch - 1,)),
            pltpu.SemaphoreType.DMA((n_batch - 1,)),
        ],
        compiler_params=pltpu.CompilerParams(
            collective_id=0, has_side_effects=True, vmem_limit_bytes=67043328
        ),
        name="block",
    )(
        norm_gain.reshape(1, -1),
        span_lengths,
        positives,
        queries[0],
        keys[0],
        values[0],
        residual[0],
        out_weight,
        source_queue,
    )
    return (anchors[None], losses)


def solution(mesh):
    return jax.shard_map(
        body,
        mesh=mesh,
        in_specs=(
            P("batch", "seq", None),
            P("batch", "seq", None),
            P("batch", "seq", None),
            P("batch", "seq", None),
            P(),
            P(),
            P("batch", None),
            P("batch", None),
            P(None, "seq"),
        ),
        out_specs=(P("batch", "seq", None), P("batch", "seq")),
        check_vma=False,
    )
```

```python
import functools
import math

import jax
import jax.numpy as jnp
from jax import lax
from jax.experimental import pallas as pl
from jax.experimental.pallas import tpu as pltpu
from jax.sharding import PartitionSpec as P

HEADS = 16
WINDOW = 512
MESH = pl.DeviceIdType.MESH
F32 = jnp.float32
BF16 = jnp.bfloat16


logit_scale = 20.0


NEVER = -1e30


def scores_to_partial(query_chunk, key_ref, value_t, blocks_apart, head_size):
    tok_rows, width = query_chunk.shape
    half = tok_rows // 2
    to_log2 = math.log2(math.e) / math.sqrt(head_size)
    lane = lax.broadcasted_iota(jnp.int32, (tok_rows, width), 1)
    query_less_key = lax.broadcasted_iota(jnp.int32, (half, half), 1) - lax.broadcasted_iota(
        jnp.int32, (half, half), 0
    )
    mixed, peaks, totals = [], [], []
    for h in range(width // head_size):
        own = (lane >= h * head_size) & (lane < (h + 1) * head_size)
        query_h = jnp.where(own, query_chunk, jnp.zeros_like(query_chunk))
        mixed_h, peaks_h, totals_h = [], [], []
        for i in range(2):
            offsets = [blocks_apart * tok_rows + (i - j) * half for j in range(2)]
            seen = [j for j in range(2) if -half < offsets[j] < WINDOW + half - 1]
            first, last = seen[0] * half, (seen[-1] + 1) * half
            scores = lax.dot_general(
                key_ref[first:last, :],
                query_h[i * half : (i + 1) * half],
                (((1,), (1,)), ((), ())),
                preferred_element_type=F32,
            )
            parts = []
            for j in seen:
                part = scores[j * half - first : (j + 1) * half - first]
                if offsets[j] < half - 1:
                    part = jnp.where(query_less_key >= -offsets[j], part, NEVER)
                if offsets[j] + half - 1 >= WINDOW:
                    part = jnp.where(query_less_key < WINDOW - offsets[j], part, NEVER)
                parts.append(part)
            peak = functools.reduce(
                jnp.maximum, [jnp.max(part, axis=0, keepdims=True) for part in parts]
            )
            parts = [jnp.exp2((part - peak) * to_log2) for part in parts]
            totals_h.append(sum(jnp.sum(part, axis=0, keepdims=True) for part in parts))
            peaks_h.append(peak)
            mixed_h.append(
                jnp.dot(
                    value_t[h * head_size : (h + 1) * head_size, first:last],
                    jnp.concatenate([part.astype(BF16) for part in parts], axis=0),
                    preferred_element_type=F32,
                )
            )
        mixed.append(jnp.concatenate(mixed_h, axis=1))
        peaks.append(jnp.concatenate(peaks_h, axis=1))
        totals.append(jnp.concatenate(totals_h, axis=1))
    stats = jnp.concatenate(
        peaks + totals + [jnp.zeros((8 - 2 * len(peaks), tok_rows), F32)], axis=0
    )
    return jnp.concatenate(mixed, axis=0), stats


def merged(mixed_a, stats_a, mixed_b, stats_b, heads, head_size):
    to_log2 = math.log2(math.e) / math.sqrt(head_size)
    mixed, peaks, totals = [], [], []
    for h in range(heads):
        rows = slice(h * head_size, (h + 1) * head_size)
        peak_a, peak_b = stats_a[h : h + 1], stats_b[h : h + 1]
        peak = jnp.maximum(peak_a, peak_b)
        keep_a = jnp.exp2((peak_a - peak) * to_log2)
        keep_b = jnp.exp2((peak_b - peak) * to_log2)
        mixed.append(mixed_a[rows].astype(F32) * keep_a + mixed_b[rows].astype(F32) * keep_b)
        totals.append(
            stats_a[heads + h : heads + h + 1] * keep_a
            + stats_b[heads + h : heads + h + 1] * keep_b
        )
        peaks.append(peak)
    return mixed, peaks, totals


def block_kernel(
    n_seq,
    n_batch,
    head_size,
    gain_ref,
    lengths_ref,
    wanted_ref,
    queries_hbm,
    keys_hbm,
    values_hbm,
    residual_hbm,
    weight_hbm,
    queue_hbm,
    anchors_ref,
    losses_ref,
    q_own,
    k_own,
    v_own,
    v_t,
    q_one,
    q_two,
    mix_own,
    stat_own,
    mix_one,
    stat_one,
    two_out,
    two_out_stat,
    two_in,
    two_in_stat,
    one_out,
    one_out_stat,
    one_in,
    one_in_stat,
    att_t,
    residual,
    weight,
    queue,
    parts,
    parts_in,
    anchors_all,
    stats,
    wanted,
    chunk_sem,
    load_sem,
    send_sem,
    recv_sem,
    part_send,
    part_recv,
    anchor_send,
    anchor_recv,
    stat_send,
    stat_recv,
):
    chunks, tok_rows, chunk_cols = q_own.shape
    heads = chunk_cols // head_size
    own_rows, width = anchors_ref.shape
    funcs = own_rows * n_seq
    seq = lax.axis_index("seq")
    batch = lax.axis_index("batch")

    def load(which, g):
        source = (queries_hbm, keys_hbm, values_hbm)[which]
        target = (q_own, k_own, v_own)[which]
        cols = pl.ds(pl.multiple_of(g * chunk_cols, chunk_cols), chunk_cols)
        return pltpu.make_async_copy(
            source.at[:, cols], target.at[g], chunk_sem.at[which, g]
        )

    def start_loads(g, carry):
        for which in range(3):
            load(which, g).start()
        return carry

    lax.fori_loop(0, chunks, start_loads, 0)
    residual_load = pltpu.make_async_copy(residual_hbm, residual, load_sem.at[0])
    weight_load = pltpu.make_async_copy(weight_hbm, weight, load_sem.at[1])
    queue_load = pltpu.make_async_copy(queue_hbm, queue, load_sem.at[2])
    residual_load.start()
    weight_load.start()
    queue_load.start()

    rows = n_batch * own_rows
    spread_at = lax.broadcasted_iota(jnp.int32, (own_rows, rows), 1)
    spread = (
        lax.rem(spread_at, own_rows) == lax.broadcasted_iota(jnp.int32, (own_rows, rows), 0)
    )
    spread = jnp.where(spread, 1.0, 0.0).astype(BF16)
    high = wanted_ref[...] // 128
    low = wanted_ref[...] - high * 128
    whole = 128.0 * jnp.dot(
        high.astype(F32).astype(BF16), spread, preferred_element_type=F32
    ) + jnp.dot(low.astype(F32).astype(BF16), spread, preferred_element_type=F32)
    mine = lax.broadcasted_iota(jnp.int32, (n_batch, rows), 1) // own_rows
    mine = mine == lax.broadcasted_iota(jnp.int32, (n_batch, rows), 0)
    wanted[...] = jnp.sum(jnp.where(mine, whole, 0.0), axis=0, keepdims=True).astype(jnp.int32)

    seq_peers = [lax.rem(seq + d, n_seq) for d in range(1, n_seq)]
    batch_peers = [lax.rem(batch + d, n_batch) for d in range(1, n_batch)]
    barrier = pltpu.get_barrier_semaphore()
    for peer in seq_peers:
        pl.semaphore_signal(barrier, inc=1, device_id={"seq": peer}, device_id_type=MESH)
    for peer in batch_peers:
        pl.semaphore_signal(barrier, inc=1, device_id={"batch": peer}, device_id_type=MESH)
    pl.semaphore_wait(barrier, n_seq - 1 + n_batch - 1)

    left = lax.rem(seq + n_seq - 1, n_seq)
    right = lax.rem(seq + 1, n_seq)
    has_left = seq >= 1
    has_right = seq <= n_seq - 2
    has_right_two = seq <= n_seq - 3

    def remote(kind, source, target, g, peer):
        return pltpu.make_async_remote_copy(
            src_ref=source.at[g],
            dst_ref=target.at[g],
            send_sem=send_sem.at[kind, g],
            recv_sem=recv_sem.at[kind, g],
            device_id={"seq": peer},
            device_id_type=MESH,
        )

    def ask_one(g):
        return remote(0, q_own, q_one, g, left)

    def ask_two(g):
        return remote(1, q_one, q_two, g, left)

    def give_two(g):
        return (
            remote(2, two_out, two_in, g, right),
            remote(3, two_out_stat, two_in_stat, g, right),
        )

    def give_one(g):
        return (
            remote(4, one_out, one_in, g, right),
            remote(5, one_out_stat, one_in_stat, g, right),
        )

    ahead = min(3, chunks)
    for g in range(ahead):
        load(0, g).wait()

        @pl.when(has_left)
        def _():
            ask_one(g).start()

    lead = min(2, chunks)

    def prepare(g):
        load(1, g).wait()
        load(2, g).wait()
        v_t[g] = v_own[g].T

    def attend_own(g):
        mix_own[g], stat_own[g] = scores_to_partial(
            q_own[g], k_own.at[g], v_t.at[g], 0, head_size
        )

    def attend_one(g):
        mix_one[g], stat_one[g] = scores_to_partial(
            q_one[g], k_own.at[g], v_t.at[g], 1, head_size
        )

    def attend_two(g):
        mixed, stat = scores_to_partial(q_two[g], k_own.at[g], v_t.at[g], 2, head_size)
        two_out[g] = mixed.astype(BF16)
        two_out_stat[g] = stat

    for g in range(lead):
        prepare(g)
    for g in range(lead):
        attend_own(g)

    def blank_one(g, carry):
        q_one[g] = jnp.zeros((tok_rows, chunk_cols), BF16)
        return carry

    def blank_two(g, carry):
        q_two[g] = jnp.zeros((tok_rows, chunk_cols), BF16)
        return carry

    @pl.when(jnp.logical_not(has_right))
    def _():
        lax.fori_loop(0, chunks, blank_one, 0)

    @pl.when(jnp.logical_not(has_right_two))
    def _():
        lax.fori_loop(0, chunks, blank_two, 0)

    def step(t, carry):
        fresh = t < chunks

        @pl.when(fresh & has_right)
        def _():
            ask_one(t).wait_recv()

            @pl.when(has_left)
            def _():
                ask_two(t).start()

        @pl.when(t + ahead < chunks)
        def _():
            load(0, t + ahead).wait()

            @pl.when(has_left)
            def _():
                ask_one(t + ahead).start()

        @pl.when(t + lead < chunks)
        def _():
            prepare(t + lead)

        @pl.when((t >= 4) & (t < chunks + 4) & has_right)
        def _():
            g = t - 4

            @pl.when(has_left)
            def _():
                for copy in give_two(g):
                    copy.wait_recv()
                mixed, peaks, totals = merged(
                    mix_one[g], stat_one[g], two_in[g], two_in_stat[g], heads, head_size
                )
                one_out[g] = jnp.concatenate(mixed, axis=0).astype(BF16)
                one_out_stat[g] = jnp.concatenate(
                    peaks + totals + [jnp.zeros((8 - 2 * heads, tok_rows), F32)], axis=0
                )

            @pl.when(jnp.logical_not(has_left))
            def _():
                one_out[g] = mix_one[g].astype(BF16)
                one_out_stat[g] = stat_one[g]

            for copy in give_one(g):
                copy.start()

        @pl.when(t < 2)
        def _():
            attend_one(t)
            attend_own(jnp.minimum(t + lead, chunks - 1))

        twice = (t >= 2) & (t < chunks + 2) & has_right_two

        @pl.when(twice)
        def _():
            ask_two(t - 2).wait_recv()

        @pl.when((t >= 2) & fresh)
        def _():
            attend_one(t)
            attend_two(t - 2)
            attend_own(jnp.minimum(t + lead, chunks - 1))

        @pl.when((t >= chunks) & (t < chunks + 2))
        def _():
            attend_two(t - 2)

        @pl.when(twice)
        def _():
            for copy in give_two(t - 2):
                copy.start()

        @pl.when((t >= 6) & (t < chunks + 6))
        def _():
            g = t - 6

            @pl.when(has_left)
            def _():
                for copy in give_one(g):
                    copy.wait_recv()
                mixed, peaks, totals = merged(
                    mix_own[g], stat_own[g], one_in[g], one_in_stat[g], heads, head_size
                )
                att_t[g] = jnp.concatenate(
                    [m / l for m, l in zip(mixed, totals)], axis=0
                ).astype(BF16)

            @pl.when(jnp.logical_not(has_left))
            def _():
                for h in range(heads):
                    rows = slice(h * head_size, (h + 1) * head_size)
                    att_t[g, rows, :] = (
                        mix_own[g, rows, :] / stat_own[g, heads + h : heads + h + 1, :]
                    ).astype(BF16)

        return carry

    lax.fori_loop(0, chunks + 6, step, 0)

    residual_load.wait()
    weight_load.wait()
    hidden = residual[...].astype(F32) + lax.dot_general(
        att_t[...].reshape(width, tok_rows),
        weight[...],
        (((0,), (0,)), ((), ())),
        preferred_element_type=F32,
    )
    scale = lax.rsqrt(jnp.mean(hidden * hidden, axis=-1, keepdims=True) + 1e-05)
    normed = (hidden * scale * gain_ref[...]).astype(BF16)

    row_ids = lax.broadcasted_iota(jnp.int32, (funcs, funcs), 0)
    func_ids = lax.broadcasted_iota(jnp.int32, (funcs, funcs), 1)
    listed = lax.rem(row_ids, own_rows) * n_seq + row_ids // own_rows
    lengths = jnp.broadcast_to(lengths_ref[...].astype(F32), (funcs, funcs))
    begin_at = jnp.sum(jnp.where(func_ids < listed, lengths, 0.0), axis=1, keepdims=True)
    end_at = jnp.sum(jnp.where(func_ids <= listed, lengths, 0.0), axis=1, keepdims=True)
    pos = (
        seq * tok_rows + lax.broadcasted_iota(jnp.int32, (funcs, tok_rows), 1)
    ).astype(F32)
    member = jnp.where((pos >= begin_at) & (pos < end_at), 1.0, 0.0).astype(BF16)
    partial = jnp.dot(member, normed, preferred_element_type=F32)
    parts[...] = partial.reshape(n_seq, own_rows, width).astype(BF16)

    copies = []
    for d in range(1, n_seq):
        copy = pltpu.make_async_remote_copy(
            src_ref=parts.at[seq_peers[d - 1]],
            dst_ref=parts_in.at[d - 1],
            send_sem=part_send.at[d - 1],
            recv_sem=part_recv.at[d - 1],
            device_id={"seq": seq_peers[d - 1]},
            device_id_type=MESH,
        )
        copy.start()
        copies.append(copy)
    pooled = parts[seq].astype(F32)
    for d in range(1, n_seq):
        copies[d - 1].wait_recv()
        pooled = pooled + parts_in[d - 1].astype(F32)
    anchors = (
        pooled * lax.rsqrt(jnp.sum(pooled * pooled, axis=-1, keepdims=True) + 1e-06)
    ).astype(BF16)
    anchors_ref[...] = anchors
    anchors_all[batch] = anchors
    for copy in copies:
        copy.wait_send()

    copies = []
    for d in range(1, n_batch):
        copy = pltpu.make_async_remote_copy(
            src_ref=anchors_all.at[batch],
            dst_ref=anchors_all.at[batch],
            send_sem=anchor_send.at[d - 1],
            recv_sem=anchor_recv.at[d - 1],
            device_id={"batch": batch_peers[d - 1]},
            device_id_type=MESH,
        )
        copy.start()
        copies.append(copy)

    def drain(g, carry):
        @pl.when(has_left)
        def _():
            ask_one(g).wait_send()

            @pl.when(has_right)
            def _():
                ask_two(g).wait_send()

        @pl.when(has_right_two)
        def _():
            for copy in give_two(g):
                copy.wait_send()

        @pl.when(has_right)
        def _():
            for copy in give_one(g):
                copy.wait_send()

        return carry

    lax.fori_loop(0, chunks, drain, 0)
    queue_load.wait()
    for copy in copies:
        copy.wait()
    logits = logit_scale * lax.dot_general(
        queue[...],
        anchors_all[...].reshape(rows, width),
        (((1,), (1,)), ((), ())),
        preferred_element_type=F32,
    )
    queue_rows = queue.shape[0]
    queue_ids = batch * queue_rows + lax.broadcasted_iota(jnp.int32, logits.shape, 0)
    row_peak = jnp.max(logits, axis=0, keepdims=True)
    row_total = jnp.sum(jnp.exp(logits - row_peak), axis=0, keepdims=True)
    positive = jnp.sum(
        jnp.where(wanted[...] == queue_ids, logits, 0.0), axis=0, keepdims=True
    )
    stats[batch] = jnp.concatenate(
        [row_peak, row_total, positive, jnp.zeros((5, rows), F32)], axis=0
    )
    copies = []
    for d in range(1, n_batch):
        copy = pltpu.make_async_remote_copy(
            src_ref=stats.at[batch],
            dst_ref=stats.at[batch],
            send_sem=stat_send.at[d - 1],
            recv_sem=stat_recv.at[d - 1],
            device_id={"batch": batch_peers[d - 1]},
            device_id_type=MESH,
        )
        copy.start()
        copies.append(copy)
    for copy in copies:
        copy.wait()
    peaks = [stats[b, 0:1, :] for b in range(n_batch)]
    top = functools.reduce(jnp.maximum, peaks)
    total = sum(stats[b, 1:2, :] * jnp.exp(peaks[b] - top) for b in range(n_batch))
    chosen = sum(stats[b, 2:3, :] for b in range(n_batch))
    loss = top + jnp.log(total) - chosen
    loss_col = jnp.sum(
        jnp.where(
            lax.broadcasted_iota(jnp.int32, (own_rows, rows), 1)
            == batch * own_rows + lax.broadcasted_iota(jnp.int32, (own_rows, rows), 0),
            jnp.broadcast_to(loss, (own_rows, rows)),
            0.0,
        ),
        axis=1,
        keepdims=True,
    )
    square = (own_rows, own_rows)
    diagonal = lax.broadcasted_iota(jnp.int32, square, 0) == lax.broadcasted_iota(
        jnp.int32, square, 1
    )
    losses_ref[...] = jnp.sum(
        jnp.where(diagonal, jnp.broadcast_to(loss_col, square), 0.0), axis=0, keepdims=True
    )


def body(
    queries, keys, values, residual, out_weight, norm_gain, source_queue, span_lengths, positives
):
    tok_rows, width = queries.shape[1:]
    head_size = width // HEADS
    n_seq = lax.axis_size("seq")
    n_batch = lax.axis_size("batch")
    own_rows = positives.shape[1]
    rows = n_batch * own_rows
    chunk_cols = 128
    chunks = width // chunk_cols
    assert (WINDOW - 1) // tok_rows + 1 == 2 and chunk_cols % head_size == 0
    vmem = pl.BlockSpec(memory_space=pltpu.VMEM)
    hbm = pl.BlockSpec(memory_space=pl.ANY)
    rows_bf16 = pltpu.VMEM((chunks, tok_rows, chunk_cols), BF16)
    cols_bf16 = pltpu.VMEM((chunks, chunk_cols, tok_rows), BF16)
    cols_f32 = pltpu.VMEM((chunks, chunk_cols, tok_rows), F32)
    stat_f32 = pltpu.VMEM((chunks, 8, tok_rows), F32)
    anchors, losses = pl.pallas_call(
        functools.partial(block_kernel, n_seq, n_batch, head_size),
        out_shape=(
            jax.ShapeDtypeStruct((own_rows, width), BF16),
            jax.ShapeDtypeStruct((1, own_rows), F32),
        ),
        in_specs=[vmem] * 3 + [hbm] * 6,
        out_specs=(vmem, vmem),
        scratch_shapes=[
            rows_bf16,
            rows_bf16,
            rows_bf16,
            cols_bf16,
            rows_bf16,
            rows_bf16,
            cols_f32,
            stat_f32,
            cols_f32,
            stat_f32,
            cols_bf16,
            stat_f32,
            cols_bf16,
            stat_f32,
            cols_bf16,
            stat_f32,
            cols_bf16,
            stat_f32,
            cols_bf16,
            pltpu.VMEM((tok_rows, width), BF16),
            pltpu.VMEM(out_weight.shape, BF16),
            pltpu.VMEM(source_queue.shape, BF16),
            pltpu.VMEM((n_seq, own_rows, width), BF16),
            pltpu.VMEM((n_seq - 1, own_rows, width), BF16),
            pltpu.VMEM((n_batch, own_rows, width), BF16),
            pltpu.VMEM((n_batch, 8, rows), F32),
            pltpu.VMEM((1, rows), jnp.int32),
            pltpu.SemaphoreType.DMA((3, chunks)),
            pltpu.SemaphoreType.DMA((3,)),
            pltpu.SemaphoreType.DMA((6, chunks)),
            pltpu.SemaphoreType.DMA((6, chunks)),
            pltpu.SemaphoreType.DMA((n_seq - 1,)),
            pltpu.SemaphoreType.DMA((n_seq - 1,)),
            pltpu.SemaphoreType.DMA((n_batch - 1,)),
            pltpu.SemaphoreType.DMA((n_batch - 1,)),
            pltpu.SemaphoreType.DMA((n_batch - 1,)),
            pltpu.SemaphoreType.DMA((n_batch - 1,)),
        ],
        compiler_params=pltpu.CompilerParams(
            collective_id=0, has_side_effects=True, vmem_limit_bytes=67043328
        ),
        name="block",
    )(
        norm_gain.reshape(1, -1),
        span_lengths,
        positives,
        queries[0],
        keys[0],
        values[0],
        residual[0],
        out_weight,
        source_queue,
    )
    return (anchors[None], losses)


def solution(mesh):
    return jax.shard_map(
        body,
        mesh=mesh,
        in_specs=(
            P("batch", "seq", None),
            P("batch", "seq", None),
            P("batch", "seq", None),
            P("batch", "seq", None),
            P(),
            P(),
            P("batch", None),
            P("batch", None),
            P(None, "seq"),
        ),
        out_specs=(P("batch", "seq", None), P("batch", "seq")),
        check_vma=False,
    )
```
